32 devices in a mesh: gx: 8 (over z, x), gy: 4 (over y, core).
Axes of the slice: x: 2, y: 2, z: 4, core: 2. Of those that a mesh axis runs over, the one named last changes fastest.
Arguments:
- e_start: float32 [3, 64, 256, 128], P(None, 'gx', 'gy'), may hold values from -6 to 6
- h_start: float32 [3, 64, 256, 128], P(None, 'gx', 'gy'), may hold values from -6 to 6
- adj_e_start: float32 [3, 64, 256, 128], P(None, 'gx', 'gy'), may hold values from -6 to 6
- adj_h_start: float32 [3, 64, 256, 128], P(None, 'gx', 'gy'), may hold values from -6 to 6
- eps_background: float32 [64, 256, 128], P('gx', 'gy'), may hold values from 1 to 4
- design: float32 [64, 256], P('gx', 'gy'), may hold values from 0 to 1
- design_tiles: int32 [8, 32], P('gx', 'gy'), may hold values from 0 to 1
- design_floor: int32 [1], replicated, may hold values from 8 to 104
- freq_index: int32 [8], replicated, may hold values from 0 to 31, as said below
- target: float32 [2, 8, 3, 64, 256], P(None, None, None, 'gx', 'gy'), may hold values from -6 to 6
Outputs:
- grad_design: float32 [64, 256], P('gx', 'gy')
- loss_weights: float32 [8], replicated
- e_final: float32 [3, 64, 256, 128], P(None, 'gx', 'gy')
- adj_e_final: float32 [3, 64, 256, 128], P(None, 'gx', 'gy')
The draws below stay inside these ranges and needn't reach their ends.
Inputs may be any that keep to these rules, and one draw needn't show every extreme that they name: `freq_index`: 8 distinct entries; the first and the last entry of the table are always among them.
All inputs are finite; a program needn't handle non-finite values.
Results may differ from the reference program's by a relative error of at most 0.00018.
Values sent between devices are 32-bit elements; how exact they have to be, the bound alone decides.
A program may use at most 64 MiB of HBM per device.

```python
import jax
import jax.numpy as jnp
from jax import lax

NZ = 128
K = 8
N_TABLE = 32
STEPS = 4
DZ = 16
TILE = 8
NX = 64
NY = 256


def draw_freq_index(key, part):
    middle = jax.random.permutation(jax.random.fold_in(key, 3), N_TABLE - 2)[:K - 2].astype(jnp.int32) + 1
    ends = jnp.array([0, N_TABLE - 1], jnp.int32)
    values = jnp.concatenate([ends, middle])
    order = jax.random.permutation(jax.random.fold_in(key, 5), K)
    return values[order].astype(jnp.int32)


def draw_design_tiles(key, part):
    tile_rows = NX // TILE
    tile_cols = NY // TILE
    region_rows = max(tile_rows // 2, 1)
    region_cols = max(tile_cols // 2, 1)
    first_key, second_key, third_key = jax.random.split(jax.random.fold_in(key, 7), 3)
    start_row = jax.random.randint(first_key, (), 0, tile_rows - region_rows + 1)
    start_col = jax.random.randint(second_key, (), 0, tile_cols - region_cols + 1)
    row_ids = jnp.arange(tile_rows, dtype=jnp.int32)[:, None]
    col_ids = jnp.arange(tile_cols, dtype=jnp.int32)[None, :]
    inside = (row_ids >= start_row) & (row_ids < start_row + region_rows) & (col_ids >= start_col) & (col_ids < start_col + region_cols)
    coins = jax.random.randint(third_key, (tile_rows, tile_cols), 0, 4) > 0
    return (inside & coins).astype(jnp.int32)


def block_scale(own_key, extent, cuts, smallest, top_value):
    loudness = 1.0
    for dim, blocks in cuts:
        draws = jax.random.uniform(jax.random.fold_in(jax.random.fold_in(own_key, 6), dim), (blocks,), jnp.float32, smallest / len(cuts), top_value / len(cuts))
        loudness = loudness * jnp.repeat(jnp.exp(draws), extent[dim] // blocks).reshape((-1,) + (1,) * (len(extent) - 1 - dim))
    return loudness


def normal_values(stream_key, shape, scale, bound, cuts=(), held_as=jnp.bfloat16):
    gain = block_scale(stream_key, shape, cuts, -0.22, 0.18) if cuts else 1.0
    entries = jax.random.normal(stream_key, shape, jnp.float32) * scale * gain
    return jnp.minimum(jnp.maximum(entries, -bound), bound).astype(held_as)


def setup_inputs(seed: int = 0) -> dict:
    key_list = jax.random.split(jax.random.key(seed), 11)
    return {
        "e_start": normal_values(key_list[0], (3, NX, NY, NZ), 1.0, 6.0, ((1, 8), (2, 4)), jnp.float32),
        "h_start": normal_values(key_list[1], (3, NX, NY, NZ), 1.0, 6.0, ((1, 8), (2, 4)), jnp.float32),
        "adj_e_start": normal_values(key_list[2], (3, NX, NY, NZ), 1.0, 6.0, ((1, 8), (2, 4)), jnp.float32),
        "adj_h_start": normal_values(key_list[3], (3, NX, NY, NZ), 1.0, 6.0, ((1, 8), (2, 4)), jnp.float32),
        "eps_background": jnp.clip(1.0 + 3.0 * jax.random.uniform(key_list[4], (NX, NY, NZ), jnp.float32) ** block_scale(key_list[4], (NX, NY, NZ), ((0, 8), (1, 4)), -0.2, 0.2), 1.0, 4.0),
        "design": jnp.clip(1.0 * jax.random.uniform(key_list[5], (NX, NY), jnp.float32) ** block_scale(key_list[5], (NX, NY), ((0, 8), (1, 4)), -0.2, 0.2), 0.0, 1.0),
        "design_tiles": draw_design_tiles(jax.random.fold_in(key_list[10], 71), 0),
        "design_floor": jax.random.randint(key_list[7], (1,), 8, NZ - DZ - 7).astype(jnp.int32),
        "freq_index": draw_freq_index(jax.random.fold_in(key_list[10], 71), 0),
        "target": normal_values(key_list[9], (2, K, 3, NX, NY), 1.0, 6.0, ((3, 8), (4, 4)), jnp.float32),
    }


courant = 0.5
sharpness = 4.0
contrast = 10.0
threshold = 0.5


def step_ahead(values, face_cells, along_axis):
    shifted = lax.slice_in_dim(values, 1, values.shape[along_axis], axis=along_axis)
    return jnp.concatenate([shifted, face_cells], along_axis) - values


def behind(values, face_cells, along_axis):
    shifted = lax.slice_in_dim(values, 0, values.shape[along_axis] - 1, axis=along_axis)
    return values - jnp.concatenate([face_cells, shifted], along_axis)


def zero_face(values, along_axis):
    return jnp.zeros_like(lax.slice_in_dim(values, 0, 1, axis=along_axis))


def curl_ahead(e_field, ey_face_x, ez_face_x, ex_face_y, ez_face_y):
    e_x, e_y, e_z = e_field[0], e_field[1], e_field[2]
    curl_x = step_ahead(e_z, ez_face_y, 1) - step_ahead(e_y, zero_face(e_y, 2), 2)
    curl_y = step_ahead(e_x, zero_face(e_x, 2), 2) - step_ahead(e_z, ez_face_x, 0)
    curl_z = step_ahead(e_y, ey_face_x, 0) - step_ahead(e_x, ex_face_y, 1)
    return jnp.stack([curl_x, curl_y, curl_z])


def curl_behind(h_field, hy_face_x, hz_face_x, hx_face_y, hz_face_y):
    h_x, h_y, h_z = h_field[0], h_field[1], h_field[2]
    curl_x = behind(h_z, hz_face_y, 1) - behind(h_y, zero_face(h_y, 2), 2)
    curl_y = behind(h_x, zero_face(h_x, 2), 2) - behind(h_z, hz_face_x, 0)
    curl_z = behind(h_y, hy_face_x, 0) - behind(h_x, hx_face_y, 1)
    return jnp.stack([curl_x, curl_y, curl_z])


def smooth_padded(extended):
    row_count = extended.shape[0] - 4
    first_pass = (extended[0:row_count] + 2.0 * extended[1:row_count + 1] + 3.0 * extended[2:row_count + 2]
                  + 2.0 * extended[3:row_count + 3] + extended[4:row_count + 4]) / 9.0
    col_count = first_pass.shape[1] - 4
    return (first_pass[:, 0:col_count] + 2.0 * first_pass[:, 1:col_count + 1] + 3.0 * first_pass[:, 2:col_count + 2]
            + 2.0 * first_pass[:, 3:col_count + 3] + first_pass[:, 4:col_count + 4]) / 9.0


def cell_mask(tile_flags):
    spread = tile_flags.astype(jnp.float32)[:, None, :, None] * jnp.ones((1, TILE, 1, TILE), jnp.float32)
    return spread.reshape(tile_flags.shape[0] * TILE, tile_flags.shape[1] * TILE)


def window(e_field, h_field, update_scale, angular, z_floor, source_layer, adjoint_source):
    freq_count = angular.shape[0]
    rows_x, rows_y = e_field.shape[1], e_field.shape[2]
    slab_re = jnp.zeros((freq_count, 3, rows_x, rows_y, DZ), jnp.float32)
    slab_im = jnp.zeros((freq_count, 3, rows_x, rows_y, DZ), jnp.float32)
    watch_re = jnp.zeros((freq_count, 3, rows_x, rows_y), jnp.float32)
    watch_im = jnp.zeros((freq_count, 3, rows_x, rows_y), jnp.float32)
    for step_index in range(STEPS):
        h_field = h_field - courant * curl_ahead(e_field, zero_face(e_field[1], 0), zero_face(e_field[2], 0),
                                                 zero_face(e_field[0], 1), zero_face(e_field[2], 1))
        e_field = e_field + update_scale[None] * curl_behind(h_field, zero_face(h_field[1], 0), zero_face(h_field[2], 0),
                                                             zero_face(h_field[0], 1), zero_face(h_field[2], 1))
        time_value = jnp.float32(step_index + 1)
        cosines = jnp.cos(angular * time_value)
        sines = jnp.sin(angular * time_value)
        if adjoint_source is not None:
            e_field = e_field + adjoint_source(cosines, sines)[..., None] * source_layer
        slab_cells = lax.dynamic_slice_in_dim(e_field, z_floor, DZ, 3)
        monitor_cells = lax.dynamic_index_in_dim(e_field, z_floor + DZ, 3, keepdims=False)
        slab_re = slab_re + cosines[:, None, None, None, None] * slab_cells[None]
        slab_im = slab_im - sines[:, None, None, None, None] * slab_cells[None]
        watch_re = watch_re + cosines[:, None, None, None] * monitor_cells[None]
        watch_im = watch_im - sines[:, None, None, None] * monitor_cells[None]
    return slab_re, slab_im, watch_re, watch_im, e_field


def reference(e_start, h_start, adj_e_start, adj_h_start, eps_background, design, design_tiles, design_floor, freq_index, target):
    z_floor = design_floor[0]
    layers = lax.iota(jnp.int32, e_start.shape[3])
    source_layer = (layers == z_floor + DZ).astype(jnp.float32)
    design_layers = ((layers >= z_floor) & (layers < z_floor + DZ)).astype(jnp.float32)
    tile_cells = cell_mask(design_tiles)
    filtered = smooth_padded(jnp.pad(design, 2))
    tilted = jnp.tanh(sharpness * (filtered - threshold))
    offset_tanh = jnp.tanh(sharpness * threshold)
    projected = (offset_tanh + tilted) / (2.0 * offset_tanh)
    gradient_slope = sharpness * (1.0 - tilted * tilted) / (2.0 * offset_tanh)
    inside = tile_cells[:, :, None] * design_layers
    permittivity = jnp.where(inside > 0.5, 1.0 + contrast * projected[:, :, None], eps_background)
    update_scale = courant / permittivity
    angular = 0.3 + 0.04 * freq_index.astype(jnp.float32)
    fwd_re, fwd_im, watch_re, watch_im, e_final = window(e_start, h_start, update_scale, angular, z_floor, source_layer, None)
    misfit_re = watch_re - target[0]
    misfit_im = watch_im - target[1]
    loss_sums = jnp.sum(misfit_re * misfit_re + misfit_im * misfit_im, axis=(1, 2, 3))
    losses = loss_sums / float(3 * NX * NY) + 1e-6
    squared = losses * losses
    weights = squared / jnp.sum(squared)

    def adjoint_source(cosines, sines):
        first = jnp.einsum("k,kcxy->cxy", weights * cosines, misfit_re, precision=lax.Precision.HIGHEST)
        second = jnp.einsum("k,kcxy->cxy", weights * sines, misfit_im, precision=lax.Precision.HIGHEST)
        return first - second

    adj_re, adj_im, unused_re, unused_im, adj_e_final = window(adj_e_start, adj_h_start, update_scale, angular, z_floor, source_layer, adjoint_source)
    product = fwd_re * adj_re - fwd_im * adj_im
    density = jnp.einsum("k,kcxyz->xyz", weights, product, precision=lax.Precision.HIGHEST)
    sensitivity = jnp.sum(density, axis=2) / float(3 * DZ)
    grad_design = smooth_padded(jnp.pad(tile_cells * gradient_slope * sensitivity, 2))
    return grad_design, weights, e_final, adj_e_final
```

```python
import functools

import jax
import jax.numpy as jnp
from jax import lax
from jax.experimental import pallas as pl
from jax.experimental.pallas import tpu as pltpu
from jax.sharding import PartitionSpec as P

STEPS = 4
DZ = 16
TILE = 8
LANES = 128

courant = 0.5
sharpness = 4.0
contrast = 10.0
threshold = 0.5

MESH = pl.DeviceIdType.MESH
F32 = jnp.float32


def when(cond):
    return pl.when(cond)


def kernel(
    nx, ny, nf, rx, ry, nz,
    floor_ref, tiles_ref, cos_ref, sin_ref, pair_ref, design_ref, target_ref,
    e_in, h_in, ae_in, ah_in, eps_in,
    grad_ref, weights_ref, e_out, ae_out,
    es, hs, eps, scale, hx, hy, plane, planes_t, source, sens, mis,
    fx, fy, part_x, part_y, gbuf,
    in_sem, out_sem, ssem, rsem, fsend, frecv, psend, precv,
):
    gx = lax.axis_index("gx")
    gy = lax.axis_index("gy")

    loads = [
        pltpu.make_async_copy(e_in, es.at[0, 0], in_sem.at[0]),
        pltpu.make_async_copy(ae_in, es.at[1, 0], in_sem.at[1]),
        pltpu.make_async_copy(h_in, hs.at[0, 0], in_sem.at[2]),
        pltpu.make_async_copy(ah_in, hs.at[1, 0], in_sem.at[3]),
        pltpu.make_async_copy(eps_in, eps, in_sem.at[4]),
    ]
    for load in loads:
        load.start()

    barrier = pltpu.get_barrier_semaphore()
    hx[...] = jnp.zeros_like(hx)
    hy[...] = jnp.zeros_like(hy)
    fx[...] = jnp.zeros_like(fx)
    fy[...] = jnp.zeros_like(fy)
    for k in range(1, nx):
        pl.semaphore_signal(barrier, inc=1, device_id=(lax.rem(gx + k, nx), gy), device_id_type=MESH)
    for k in range(1, ny):
        pl.semaphore_signal(barrier, inc=1, device_id=(gx, lax.rem(gy + k, ny)), device_id_type=MESH)

    row = lax.broadcasted_iota(jnp.int32, (ry, nz), 0)
    lane = lax.broadcasted_iota(jnp.int32, (ry, nz), 1)
    z0 = floor_ref[0]
    at_monitor = lane == z0 + DZ
    in_slab = (lane >= z0) & (lane < z0 + DZ)

    def copies(run, t, kind):
        slot = run * 2 * STEPS + 2 * t + kind
        if kind == 0:
            src, layer, rows, dx, dy = es.at[run, t], 0, pl.ds(0, 8), gx - 1, gy - 1
        else:
            src, layer, rows, dx, dy = hs.at[run, t + 1], rx - 1, pl.ds(ry - 8, 8), gx + 1, gy + 1
        in_x = pltpu.make_async_remote_copy(
            src.at[pl.ds(1, 2), layer], hx.at[slot], ssem.at[slot, 0], rsem.at[slot, 0],
            device_id=(dx, gy), device_id_type=MESH)
        in_y = [
            pltpu.make_async_remote_copy(
                src.at[2 * j, :, rows], hy.at[slot, j], ssem.at[slot, 1 + j], rsem.at[slot, 1 + j],
                device_id=(gx, dy), device_id_type=MESH)
            for j in range(2)
        ]
        return in_x, in_y

    low = (gx > 0, gy > 0)
    high = (gx < nx - 1, gy < ny - 1)

    def send_x(run, t, kind):
        @when((low, high)[kind][0])
        def _():
            copies(run, t, kind)[0].start()

    def send_y(run, t, kind):
        @when((low, high)[kind][1])
        def _():
            for copy in copies(run, t, kind)[1]:
                copy.start()

    def receive(run, t, kind):
        @when((high, low)[kind][0])
        def _():
            copies(run, t, kind)[0].wait_recv()

        @when((high, low)[kind][1])
        def _():
            for copy in copies(run, t, kind)[1]:
                copy.wait_recv()

    def finish(run, t, kind):
        @when((low, high)[kind][0])
        def _():
            copies(run, t, kind)[0].wait_send()

        @when((low, high)[kind][1])
        def _():
            for copy in copies(run, t, kind)[1]:
                copy.wait_send()

    def next_y(v, face):
        return jnp.where(row == ry - 1, face, pltpu.roll(v, ry - 1, 0))

    def next_z(v):
        return jnp.where(lane == nz - 1, 0.0, pltpu.roll(v, nz - 1, 1))

    def last_y(v, face):
        return jnp.where(row == 0, face, pltpu.roll(v, 1, 0))

    def last_z(v):
        return jnp.where(lane == 0, 0.0, pltpu.roll(v, 1, 1))

    def h_layer(run, t, i, ey_next, ez_next):
        slot = run * 2 * STEPS + 2 * t
        ex, ey, ez = (es[run, t, c, i] for c in range(3))
        face_x, face_z = hy[slot, 0, i, 0:1, :], hy[slot, 1, i, 0:1, :]
        hs[run, t + 1, 0, i] = hs[run, t, 0, i] - courant * (
            (next_y(ez, face_z) - ez) - (next_z(ey) - ey))
        hs[run, t + 1, 1, i] = hs[run, t, 1, i] - courant * ((next_z(ex) - ex) - (ez_next - ez))
        hs[run, t + 1, 2, i] = hs[run, t, 2, i] - courant * (
            (ey_next - ey) - (next_y(ex, face_x) - ex))

    def h_step(run, t):
        slot = run * 2 * STEPS + 2 * t
        receive(run, t, 0)
        h_layer(run, t, rx - 1, hx[slot, 0], hx[slot, 1])
        send_x(run, t, 1)

        def inner(i, carry):
            h_layer(run, t, i, es[run, t, 1, i + 1], es[run, t, 2, i + 1])
            return carry

        lax.fori_loop(0, rx - 1, inner, 0)
        send_y(run, t, 1)

    def column(t, c, i):
        return lane == (c * STEPS + t) * rx + i

    def e_layer(run, t, i, hy_last, hz_last, sourced):
        slot = run * 2 * STEPS + 2 * t + 1
        mx, my, mz = (hs[run, t + 1, c, i] for c in range(3))
        face_x, face_z = hy[slot, 0, i, 7:8, :], hy[slot, 1, i, 7:8, :]
        s = scale[i]
        new = [
            es[run, t, 0, i] + s * ((mz - last_y(mz, face_z)) - (my - last_z(my))),
            es[run, t, 1, i] + s * ((mx - last_z(mx)) - (mz - hz_last)),
            es[run, t, 2, i] + s * ((my - hy_last) - (mx - last_y(mx, face_x))),
        ]
        for c in range(3):
            if sourced:
                new[c] = new[c] + source_term(t, c, i)
            es[run, t + 1, c, i] = new[c]

    def source_term(t, c, i):
        value = jnp.sum(jnp.where(column(t, c, i), source[...], 0.0), axis=1, keepdims=True)
        return jnp.where(at_monitor, value, 0.0)

    def e_step(run, t, sourced, send):
        slot = run * 2 * STEPS + 2 * t + 1
        receive(run, t, 1)
        e_layer(run, t, 0, hx[slot, 0], hx[slot, 1], sourced)
        if send:
            send_x(run, t + 1, 0)

        def inner(i, carry):
            e_layer(run, t, i, hs[run, t + 1, 1, i - 1], hs[run, t + 1, 2, i - 1], sourced)
            return carry

        lax.fori_loop(1, rx, inner, 0)
        if send:
            send_y(run, t + 1, 0)

    def watch(t):
        def one(i, carry):
            total = plane[...]
            for c in range(3):
                value = jnp.sum(jnp.where(at_monitor, es[0, t + 1, c, i], 0.0), axis=1, keepdims=True)
                total = jnp.where(column(t, c, i), value, total)
            plane[...] = total
            return carry

        lax.fori_loop(0, rx, one, 0)

    def swaps(which):
        def along(buf, sems, send_to):
            return [
                pltpu.make_async_remote_copy(
                    buf.at[which, 1], buf.at[which, 2 - 2 * j], fsend.at[which, sems, j],
                    frecv.at[which, sems, j], device_id=send_to[j], device_id_type=MESH)
                for j in range(2)
            ]

        return (along(fx, 0, ((gx - 1, gy), (gx + 1, gy))), along(fy, 1, ((gx, gy - 1), (gx, gy + 1))))

    def swap_start(which, a):
        for j in range(2):
            @when((low, high)[j][a])
            def _():
                swaps(which)[a][j].start()

    def swap_wait(which, a):
        for j in range(2):
            @when((high, low)[j][a])
            def _():
                swaps(which)[a][j].wait_recv()

            @when((low, high)[j][a])
            def _():
                swaps(which)[a][j].wait_send()

    plane_lane = lax.broadcasted_iota(jnp.int32, (rx, LANES), 1)

    def filter_start(which, value):
        fx[which, 1] = value
        swap_start(which, 0)

    def filter_middle(which):
        swap_wait(which, 0)
        wide = jnp.concatenate([fx[which, 0], fx[which, 1], fx[which, 2]], 0)
        taps = [wide[rx - 2 + d: 2 * rx - 2 + d] for d in range(5)]
        fy[which, 1] = (taps[0] + 2.0 * taps[1] + 3.0 * taps[2] + 2.0 * taps[3] + taps[4]) / 9.0
        swap_start(which, 1)

    def filter_end(which):
        swap_wait(which, 1)
        below = pltpu.roll(fy[which, 0], LANES - ry, 1)
        above = pltpu.roll(fy[which, 2], ry, 1)
        wide = jnp.where(plane_lane < ry, fy[which, 1],
                         jnp.where(plane_lane < ry + 2, above,
                                   jnp.where(plane_lane >= LANES - 2, below, 0.0)))
        taps = [wide if d == 2 else pltpu.roll(wide, (2 - d) % LANES, 1) for d in range(5)]
        return (taps[0] + 2.0 * taps[1] + 3.0 * taps[2] + 2.0 * taps[3] + taps[4]) / 9.0

    pl.semaphore_wait(barrier, nx - 1 + ny - 1)
    gbuf[...] = jnp.zeros_like(gbuf)
    gbuf[0:rx, 0:ry] = design_ref[...]
    filter_start(0, gbuf[0:rx, :])
    plane[...] = jnp.zeros_like(plane)
    sens[...] = jnp.zeros_like(sens)
    for run in range(2):
        loads[run].wait()
        send_x(run, 0, 0)
        send_y(run, 0, 0)
    filter_middle(0)
    loads[2].wait()
    h_step(0, 0)
    loads[3].wait()
    h_step(1, 0)

    filtered = filter_end(0)
    tilted = jnp.tanh(sharpness * (filtered - threshold))
    offset_tanh = jnp.tanh(jnp.full((1, 1), sharpness * threshold, F32))
    projected = (offset_tanh + tilted) / (2.0 * offset_tanh)
    slope = sharpness * (1.0 - tilted * tilted) / (2.0 * offset_tanh)
    cells = jnp.zeros((rx, LANES), F32)
    for a in range(rx // TILE):
        for b in range(ry // TILE):
            x_of = lax.broadcasted_iota(jnp.int32, (rx, LANES), 0)
            here = (x_of // TILE == a) & (plane_lane // TILE == b)
            cells = jnp.where(here, tiles_ref[a, b].astype(F32), cells)
    gbuf[0:rx, :] = jnp.where(cells > 0.5, 1.0 + contrast * projected, -1.0)
    chosen = jnp.transpose(gbuf[...])[0:ry, :]
    slope = slope * cells
    loads[4].wait()
    for i in range(rx):
        value = jnp.sum(jnp.where(lane == i, chosen, 0.0), axis=1, keepdims=True)
        permittivity = jnp.where(in_slab & (value > 0.0), value, eps[i])
        scale[i] = courant / permittivity

    e_step(0, 0, False, True)
    e_step(1, 0, False, False)
    watch(0)

    def forward(t, carry):
        h_step(0, t)
        e_step(0, t, False, True)
        watch(t)
        return carry

    lax.fori_loop(1, STEPS - 1, forward, 0)
    h_step(0, STEPS - 1)
    e_step(0, STEPS - 1, False, False)
    watch(STEPS - 1)
    stores = [pltpu.make_async_copy(es.at[0, STEPS], e_out, out_sem.at[0]),
              pltpu.make_async_copy(es.at[1, STEPS], ae_out, out_sem.at[1])]
    stores[0].start()

    planes_t[...] = jnp.transpose(plane[...])

    def monitor(c, t):
        first = (c * STEPS + t) * rx
        return planes_t[first: first + rx, :]

    shown = [[monitor(c, t) for t in range(STEPS)] for c in range(3)]
    k_row = lax.broadcasted_iota(jnp.int32, (nf, LANES), 0)
    part = jnp.zeros((nf, LANES), F32)
    for k in range(nf):
        square = jnp.zeros((rx, ry), F32)
        for c in range(3):
            re = -target_ref[0, k, c]
            im = -target_ref[1, k, c]
            for t in range(STEPS):
                re = re + cos_ref[k, t] * shown[c][t]
                im = im - sin_ref[k, t] * shown[c][t]
            mis[0, k, c] = re
            mis[1, k, c] = im
            square = square + (re * re + im * im)
        total = jnp.sum(jnp.sum(square, axis=0, keepdims=True), axis=1, keepdims=True)
        part = jnp.where(k_row == k, total, part)

    def gathers(buf, axis):
        me, n = (gx, nx) if axis == 0 else (gy, ny)
        out = []
        for k in range(1, n):
            other = lax.rem(me + k, n)
            out.append(pltpu.make_async_remote_copy(
                buf.at[me], buf.at[me], psend.at[axis, k], precv.at[axis, k],
                device_id=(other, gy) if axis == 0 else (gx, other), device_id_type=MESH))
        return out

    def gather_sum(buf, axis, value):
        me, n = (gx, nx) if axis == 0 else (gy, ny)
        buf[me] = value
        for copy in gathers(buf, axis):
            copy.start()
        for copy in gathers(buf, axis):
            copy.wait()
        total = buf[0]
        for k in range(1, n):
            total = total + buf[k]
        return total

    loss_sums = gather_sum(part_y, 1, gather_sum(part_x, 0, part))
    losses = loss_sums / float(3 * rx * nx * ry * ny) + 1e-06
    squared = losses * losses
    weights = squared / jnp.sum(squared, axis=0, keepdims=True)
    weights_ref[...] = weights

    sources = [[jnp.zeros((rx, ry), F32) for _ in range(STEPS)] for _ in range(3)]
    for k in range(nf):
        w = weights[k:k + 1, 0:1]
        for c in range(3):
            re = w * mis[0, k, c]
            im = w * mis[1, k, c]
            for t in range(STEPS):
                sources[c][t] = sources[c][t] + (cos_ref[k, t] * re - sin_ref[k, t] * im)
    planes_t[...] = jnp.zeros_like(planes_t)
    for c in range(3):
        for t in range(STEPS):
            first = (c * STEPS + t) * rx
            planes_t[first: first + rx, :] = sources[c][t]
    source[...] = jnp.transpose(planes_t[...])
    mixed = jnp.sum(weights * pair_ref[...], axis=0, keepdims=True)

    def first_source(i, carry):
        for c in range(3):
            es[1, 1, c, i] = es[1, 1, c, i] + source_term(0, c, i)
        return carry

    lax.fori_loop(0, rx, first_source, 0)
    send_x(1, 1, 0)
    send_y(1, 1, 0)

    def correlate(s):
        lane_row = lax.broadcasted_iota(jnp.int32, (1, LANES), 1)
        factors = [
            jnp.sum(jnp.where(lane_row == t * STEPS + s, mixed, 0.0), axis=1, keepdims=True)
            for t in range(STEPS)
        ]

        def one(i, carry):
            total = sens[i]
            for c in range(3):
                mix = factors[0] * es[0, 1, c, i]
                for t in range(1, STEPS):
                    mix = mix + factors[t] * es[0, t + 1, c, i]
                total = total + mix * es[1, s + 1, c, i]
            sens[i] = total
            return carry

        lax.fori_loop(0, rx, one, 0)

    correlate(0)

    def adjoint(t, carry):
        h_step(1, t)
        e_step(1, t, True, True)
        correlate(t)
        return carry

    lax.fori_loop(1, STEPS - 1, adjoint, 0)
    h_step(1, STEPS - 1)
    e_step(1, STEPS - 1, True, False)
    stores[1].start()
    correlate(STEPS - 1)

    total = jnp.zeros((ry, nz), F32)
    for i in range(rx):
        value = jnp.sum(jnp.where(in_slab, sens[i], 0.0), axis=1, keepdims=True)
        total = jnp.where(lane == i, value, total)
    gbuf[...] = jnp.zeros_like(gbuf)
    gbuf[:, 0:ry] = jnp.transpose(total)
    density = gbuf[0:rx, :] / float(3 * DZ)
    filter_start(1, slope * density)
    filter_middle(1)
    grad_ref[...] = filter_end(1)[:, 0:ry]

    for run in range(2):
        for t in range(STEPS):
            for kind in range(2):
                finish(run, t, kind)
    for store in stores:
        store.wait()


def body(
    nx, ny, e_start, h_start, adj_e_start, adj_h_start, eps_background, design, design_tiles,
    design_floor, freq_index, target,
):
    rx, ry, nz = e_start.shape[1:]
    nf = freq_index.shape[0]
    angular = 0.3 + 0.04 * freq_index.astype(F32)
    times = jnp.arange(1, STEPS + 1, dtype=F32)
    phase = angular[:, None] * times[None, :]
    cosines, sines = jnp.cos(phase), jnp.sin(phase)
    pairs = cosines[:, :, None] * cosines[:, None, :] - sines[:, :, None] * sines[:, None, :]
    pairs = jnp.pad(pairs.reshape(nf, STEPS * STEPS), ((0, 0), (0, LANES - STEPS * STEPS)))
    smem = pl.BlockSpec(memory_space=pltpu.SMEM)
    vmem = pl.BlockSpec(memory_space=pltpu.VMEM)
    hbm = pl.BlockSpec(memory_space=pl.ANY)
    field = jax.ShapeDtypeStruct((3, rx, ry, nz), F32)
    slots = 4 * STEPS
    grad, weights, e_final, adj_e_final = pl.pallas_call(
        functools.partial(kernel, nx, ny, nf, rx, ry, nz),
        out_shape=(
            jax.ShapeDtypeStruct((rx, ry), F32),
            jax.ShapeDtypeStruct((nf, LANES), F32),
            field,
            field,
        ),
        in_specs=[smem, smem, smem, smem, vmem, vmem, vmem] + [hbm] * 5,
        out_specs=(vmem, vmem, hbm, hbm),
        scratch_shapes=[
            pltpu.VMEM((2, STEPS + 1, 3, rx, ry, nz), F32),
            pltpu.VMEM((2, STEPS + 1, 3, rx, ry, nz), F32),
            pltpu.VMEM((rx, ry, nz), F32),
            pltpu.VMEM((rx, ry, nz), F32),
            pltpu.VMEM((slots, 2, ry, nz), F32),
            pltpu.VMEM((slots, 2, rx, 8, nz), F32),
            pltpu.VMEM((ry, LANES), F32),
            pltpu.VMEM((LANES, ry), F32),
            pltpu.VMEM((ry, LANES), F32),
            pltpu.VMEM((rx, ry, nz), F32),
            pltpu.VMEM((2, nf, 3, rx, ry), F32),
            pltpu.VMEM((2, 3, rx, LANES), F32),
            pltpu.VMEM((2, 3, rx, LANES), F32),
            pltpu.VMEM((nx, nf, LANES), F32),
            pltpu.VMEM((ny, nf, LANES), F32),
            pltpu.VMEM((LANES, LANES), F32),
            pltpu.SemaphoreType.DMA((5,)),
            pltpu.SemaphoreType.DMA((2,)),
            pltpu.SemaphoreType.DMA((slots, 3)),
            pltpu.SemaphoreType.DMA((slots, 3)),
            pltpu.SemaphoreType.DMA((2, 2, 2)),
            pltpu.SemaphoreType.DMA((2, 2, 2)),
            pltpu.SemaphoreType.DMA((2, max(nx, ny))),
            pltpu.SemaphoreType.DMA((2, max(nx, ny))),
        ],
        compiler_params=pltpu.CompilerParams(
            collective_id=0, has_side_effects=True, vmem_limit_bytes=48 << 20
        ),
    )(
        design_floor, design_tiles, cosines, sines, pairs, design, target,
        e_start, h_start, adj_e_start, adj_h_start, eps_background,
    )
    return grad, weights[:, 0], e_final, adj_e_final


def solution(mesh):
    placed = (
        P(None, "gx", "gy", None),
        P(None, "gx", "gy", None),
        P(None, "gx", "gy", None),
        P(None, "gx", "gy", None),
        P("gx", "gy", None),
        P("gx", "gy"),
        P("gx", "gy"),
        P(),
        P(),
        P(None, None, None, "gx", "gy"),
    )
    return jax.shard_map(
        functools.partial(body, mesh.shape["gx"], mesh.shape["gy"]),
        mesh=mesh,
        in_specs=placed,
        out_specs=(P("gx", "gy"), P(), P(None, "gx", "gy", None), P(None, "gx", "gy", None)),
        check_vma=False,
    )
```

```python
import functools

import jax
import jax.numpy as jnp
from jax import lax
from jax.experimental import pallas as pl
from jax.experimental.pallas import tpu as pltpu
from jax.sharding import PartitionSpec as P

STEPS = 4
DZ = 16
TILE = 8
LANES = 128

courant = 0.5
sharpness = 4.0
contrast = 10.0
threshold = 0.5

MESH = pl.DeviceIdType.MESH
F32 = jnp.float32


def when(cond):
    return pl.when(cond)


def kernel(
    nx, ny, nf, rx, ry, nz,
    floor_ref, tiles_ref, cos_ref, sin_ref, pair_ref, design_ref, target_ref,
    e_in, h_in, ae_in, ah_in, eps_in,
    grad_ref, weights_ref, e_out, ae_out,
    es, hs, eps, scale, hx, hy, plane, planes_t, sens, mis,
    fx, near_scale, near_source, reply, reply_t, part_x, part_y, gbuf,
    in_sem, out_sem, ssem, rsem, fsend, frecv, psend, precv,
):
    gx = lax.axis_index("gx")
    gy = lax.axis_index("gy")

    loads = [
        pltpu.make_async_copy(e_in, es.at[0, 0], in_sem.at[0]),
        pltpu.make_async_copy(ae_in, es.at[1, 0], in_sem.at[1]),
        pltpu.make_async_copy(h_in, hs.at[0, 0], in_sem.at[2]),
        pltpu.make_async_copy(ah_in, hs.at[1, 0], in_sem.at[3]),
        pltpu.make_async_copy(eps_in, eps, in_sem.at[4]),
    ]
    for load in loads:
        load.start()

    barrier = pltpu.get_barrier_semaphore()
    hx[...] = jnp.zeros_like(hx)
    hy[...] = jnp.zeros_like(hy)
    fx[...] = jnp.zeros_like(fx)
    near_scale[...] = jnp.zeros_like(near_scale)
    near_source[...] = jnp.zeros_like(near_source)
    reply[...] = jnp.zeros_like(reply)
    for k in range(1, nx):
        pl.semaphore_signal(barrier, inc=1, device_id=(lax.rem(gx + k, nx), gy), device_id_type=MESH)
    for k in range(1, ny):
        pl.semaphore_signal(barrier, inc=1, device_id=(gx, lax.rem(gy + k, ny)), device_id_type=MESH)

    corners = [(dx, dy) for dx in (-1, 1) for dy in (-1, 1)]
    around = [(-1, 0), (1, 0), (0, -1), (0, 1)] + corners

    def there(dx, dy):
        return (gx + dx >= 0) & (gx + dx < nx) & (gy + dy >= 0) & (gy + dy < ny)

    for dx, dy in corners:
        @when(there(dx, dy))
        def _():
            pl.semaphore_signal(barrier, inc=1, device_id=(gx + dx, gy + dy), device_id_type=MESH)

    row = lax.broadcasted_iota(jnp.int32, (ry, nz), 0)
    lane = lax.broadcasted_iota(jnp.int32, (ry, nz), 1)
    z0 = floor_ref[0]
    at_monitor = lane == z0 + DZ
    in_slab = (lane >= z0) & (lane < z0 + DZ)

    def copies(run, t, kind):
        slot = run * 2 * STEPS + 2 * t + kind
        if kind == 0:
            src, layer, rows, dx, dy = es.at[run, t], 0, pl.ds(0, 8), gx - 1, gy - 1
        else:
            src, layer, rows, dx, dy = hs.at[run, t + 1], rx - 1, pl.ds(ry - 8, 8), gx + 1, gy + 1
        in_x = lambda: pltpu.make_async_remote_copy(
            src.at[pl.ds(1, 2), layer], hx.at[slot], ssem.at[slot, 0], rsem.at[slot, 0],
            device_id=(dx, gy), device_id_type=MESH)
        in_y = lambda: [
            pltpu.make_async_remote_copy(
                src.at[2 * j, :, rows], hy.at[slot, j], ssem.at[slot, 1 + j], rsem.at[slot, 1 + j],
                device_id=(gx, dy), device_id_type=MESH)
            for j in range(2)
        ]
        return in_x, in_y

    low = (gx > 0, gy > 0)
    high = (gx < nx - 1, gy < ny - 1)

    def send_x(run, t, kind):
        @when((low, high)[kind][0])
        def _():
            copies(run, t, kind)[0]().start()

    def send_y(run, t, kind):
        @when((low, high)[kind][1])
        def _():
            for copy in copies(run, t, kind)[1]():
                copy.start()

    def receive(run, t, kind):
        @when((high, low)[kind][0])
        def _():
            copies(run, t, kind)[0]().wait_recv()

        @when((high, low)[kind][1])
        def _():
            for copy in copies(run, t, kind)[1]():
                copy.wait_recv()

    def finish(run, t, kind):
        @when((low, high)[kind][0])
        def _():
            copies(run, t, kind)[0]().wait_send()

        @when((low, high)[kind][1])
        def _():
            for copy in copies(run, t, kind)[1]():
                copy.wait_send()

    def next_y(v, face):
        return jnp.where(row == ry - 1, face, pltpu.roll(v, ry - 1, 0))

    def next_z(v):
        return jnp.where(lane == nz - 1, 0.0, pltpu.roll(v, nz - 1, 1))

    def last_y(v, face):
        return jnp.where(row == 0, face, pltpu.roll(v, 1, 0))

    def last_z(v):
        return jnp.where(lane == 0, 0.0, pltpu.roll(v, 1, 1))

    def h_layer(run, t, i, ey_next, ez_next):
        slot = run * 2 * STEPS + 2 * t
        ex, ey, ez = (es[run, t, c, i] for c in range(3))
        face_x, face_z = hy[slot, 0, i, 0:1, :], hy[slot, 1, i, 0:1, :]
        hs[run, t + 1, 0, i] = hs[run, t, 0, i] - courant * (
            (next_y(ez, face_z) - ez) - (next_z(ey) - ey))
        hs[run, t + 1, 1, i] = hs[run, t, 1, i] - courant * ((next_z(ex) - ex) - (ez_next - ez))
        hs[run, t + 1, 2, i] = hs[run, t, 2, i] - courant * (
            (ey_next - ey) - (next_y(ex, face_x) - ex))

    def h_step(run, t):
        slot = run * 2 * STEPS + 2 * t
        receive(run, t, 0)
        h_layer(run, t, rx - 1, hx[slot, 0], hx[slot, 1])
        send_x(run, t, 1)

        def inner(i, carry):
            h_layer(run, t, i, es[run, t, 1, i + 1], es[run, t, 2, i + 1])
            return carry

        lax.fori_loop(0, rx - 1, inner, 0, unroll=True)
        send_y(run, t, 1)

    def column(t, c, i):
        return lane == (c * STEPS + t) * rx + i

    def e_layer(run, t, i, hy_last, hz_last):
        slot = run * 2 * STEPS + 2 * t + 1
        mx, my, mz = (hs[run, t + 1, c, i] for c in range(3))
        face_x, face_z = hy[slot, 0, i, 7:8, :], hy[slot, 1, i, 7:8, :]
        s = scale[i]
        new = [
            es[run, t, 0, i] + s * ((mz - last_y(mz, face_z)) - (my - last_z(my))),
            es[run, t, 1, i] + s * ((mx - last_z(mx)) - (mz - hz_last)),
            es[run, t, 2, i] + s * ((my - hy_last) - (mx - last_y(mx, face_x))),
        ]
        for c in range(3):
            es[run, t + 1, c, i] = new[c]

    def e_step(run, t, send):
        slot = run * 2 * STEPS + 2 * t + 1
        receive(run, t, 1)
        e_layer(run, t, 0, hx[slot, 0], hx[slot, 1])
        if send:
            send_x(run, t + 1, 0)

        def inner(i, carry):
            e_layer(run, t, i, hs[run, t + 1, 1, i - 1], hs[run, t + 1, 2, i - 1])
            return carry

        lax.fori_loop(1, rx, inner, 0, unroll=True)
        if send:
            send_y(run, t + 1, 0)

    def watch(t):
        def one(i, carry):
            total = plane[...]
            for c in range(3):
                value = jnp.sum(jnp.where(at_monitor, es[0, t + 1, c, i], 0.0), axis=1, keepdims=True)
                total = jnp.where(column(t, c, i), value, total)
            plane[...] = total
            return carry

        lax.fori_loop(0, rx, one, 0, unroll=True)

    def spread_copy(buf, which, n):
        dx, dy = around[n]
        return pltpu.make_async_remote_copy(
            buf.at[1, 1], buf.at[1 - dx, 1 - dy], fsend.at[which, n], frecv.at[which, n],
            device_id=(gx + dx, gy + dy), device_id_type=MESH)

    def spread(buf, which):
        for n, (dx, dy) in enumerate(around):
            @when(there(dx, dy))
            def _():
                spread_copy(buf, which, n).start()

    def gathered(buf, which):
        for n, (dx, dy) in enumerate(around):
            @when(there(-dx, -dy))
            def _():
                spread_copy(buf, which, n).wait_recv()

            @when(there(dx, dy))
            def _():
                spread_copy(buf, which, n).wait_send()

    plane_lane = lax.broadcasted_iota(jnp.int32, (rx, LANES), 1)

    def widen(block):
        rows = []
        for a in range(3):
            below = pltpu.roll(block(a, 0), LANES - ry, 1)
            above = pltpu.roll(block(a, 2), ry, 1)
            rows.append(jnp.where(plane_lane < ry, block(a, 1),
                        jnp.where(plane_lane < ry + 4, above,
                        jnp.where(plane_lane >= LANES - 4, below, 0.0))))
        return jnp.concatenate(rows, 0)

    def smooth(wide):
        taps = [wide[rx - 2 + d: 2 * rx - 2 + d] for d in range(5)]
        first = (taps[0] + 2.0 * taps[1] + 3.0 * taps[2] + 2.0 * taps[3] + taps[4]) / 9.0
        taps = [first if d == 2 else pltpu.roll(first, (2 - d) % LANES, 1) for d in range(5)]
        return (taps[0] + 2.0 * taps[1] + 3.0 * taps[2] + 2.0 * taps[3] + taps[4]) / 9.0

    beside_x = (gx > 0).astype(jnp.int32) + (gx < nx - 1).astype(jnp.int32)
    beside_y = (gy > 0).astype(jnp.int32) + (gy < ny - 1).astype(jnp.int32)
    pl.semaphore_wait(barrier, nx - 1 + ny - 1 + beside_x * beside_y)
    gbuf[...] = jnp.zeros_like(gbuf)
    gbuf[0:rx, 0:ry] = design_ref[...]
    fx[0, 1, 1] = gbuf[0:rx, :]
    spread(fx.at[0], 0)
    plane[...] = jnp.zeros_like(plane)
    sens[...] = jnp.zeros_like(sens)
    for run in range(2):
        loads[run].wait()
        send_x(run, 0, 0)
        send_y(run, 0, 0)
    loads[2].wait()
    h_step(0, 0)
    loads[3].wait()
    h_step(1, 0)

    gathered(fx.at[0], 0)
    filtered = smooth(widen(lambda a, b: fx[0, a, b]))
    tilted = jnp.tanh(sharpness * (filtered - threshold))
    offset_tanh = jnp.tanh(jnp.full((1, 1), sharpness * threshold, F32))
    projected = (offset_tanh + tilted) / (2.0 * offset_tanh)
    slope = sharpness * (1.0 - tilted * tilted) / (2.0 * offset_tanh)
    cells = jnp.zeros((rx, LANES), F32)
    for a in range(rx // TILE):
        for b in range(ry // TILE):
            x_of = lax.broadcasted_iota(jnp.int32, (rx, LANES), 0)
            here = (x_of // TILE == a) & (plane_lane // TILE == b)
            cells = jnp.where(here, tiles_ref[a, b].astype(F32), cells)
    gbuf[0:rx, :] = jnp.where(cells > 0.5, 1.0 + contrast * projected, -1.0)
    chosen = jnp.transpose(gbuf[...])[0:ry, :]
    slope = slope * cells
    loads[4].wait()
    for i in range(rx):
        value = jnp.sum(jnp.where(lane == i, chosen, 0.0), axis=1, keepdims=True)
        permittivity = jnp.where(in_slab & (value > 0.0), value, eps[i])
        scale[i] = courant / permittivity

    e_step(0, 0, True)
    e_step(1, 0, True)
    watch(0)

    reach = STEPS - 1
    spans = 2 * reach + 1
    z_low = z0 + DZ - reach
    total = jnp.zeros((ry, nz), F32)
    for j in range(spans):
        for i in range(rx):
            value = jnp.sum(jnp.where(lane == z_low + j, scale[i], 0.0), axis=1, keepdims=True)
            total = jnp.where(lane == j * rx + i, value, total)
    planes_t[...] = jnp.transpose(total)
    for j in range(spans):
        near_scale[1, 1, j, :, 0:ry] = planes_t[j * rx: (j + 1) * rx, :]
    spread(near_scale, 2)

    def both(t, carry):
        h_step(0, t)
        h_step(1, t)
        e_step(0, t, True)
        e_step(1, t, True)
        watch(t)
        return carry

    lax.fori_loop(1, STEPS - 1, both, 0)
    h_step(0, STEPS - 1)
    h_step(1, STEPS - 1)
    e_step(0, STEPS - 1, False)
    watch(STEPS - 1)
    stores = [pltpu.make_async_copy(es.at[0, STEPS], e_out, out_sem.at[0]),
              pltpu.make_async_copy(es.at[1, STEPS], ae_out, out_sem.at[1])]
    stores[0].start()

    planes_t[...] = jnp.transpose(plane[...])

    def monitor(c, t):
        first = (c * STEPS + t) * rx
        return planes_t[first: first + rx, :]

    shown = [[monitor(c, t) for t in range(STEPS)] for c in range(3)]
    k_row = lax.broadcasted_iota(jnp.int32, (nf, LANES), 0)
    part = jnp.zeros((nf, LANES), F32)
    for k in range(nf):
        square = jnp.zeros((rx, ry), F32)
        for c in range(3):
            re = -target_ref[0, k, c]
            im = -target_ref[1, k, c]
            for t in range(STEPS):
                re = re + cos_ref[k, t] * shown[c][t]
                im = im - sin_ref[k, t] * shown[c][t]
            mis[0, k, c] = re
            mis[1, k, c] = im
            square = square + (re * re + im * im)
        total = jnp.sum(jnp.sum(square, axis=0, keepdims=True), axis=1, keepdims=True)
        part = jnp.where(k_row == k, total, part)

    def gathers(buf, axis):
        me, n = (gx, nx) if axis == 0 else (gy, ny)
        out = []
        for k in range(1, n):
            other = lax.rem(me + k, n)
            out.append(pltpu.make_async_remote_copy(
                buf.at[me], buf.at[me], psend.at[axis, k], precv.at[axis, k],
                device_id=(other, gy) if axis == 0 else (gx, other), device_id_type=MESH))
        return out

    def gather_start(buf, axis, value):
        buf[(gx, gy)[axis]] = value
        for copy in gathers(buf, axis):
            copy.start()

    def gather_sum(buf, axis):
        for copy in gathers(buf, axis):
            copy.wait()
        total = buf[0]
        for k in range(1, (nx, ny)[axis]):
            total = total + buf[k]
        return total

    gather_start(part_x, 0, part)
    e_step(1, STEPS - 1, False)
    gather_start(part_y, 1, gather_sum(part_x, 0))
    gathered(near_scale, 2)
    scales = [widen(lambda a, b: near_scale[a, b, j]) for j in range(spans)]
    loss_sums = gather_sum(part_y, 1)
    losses = loss_sums / float(3 * rx * nx * ry * ny) + 1e-06
    squared = losses * losses
    weights = squared / jnp.sum(squared, axis=0, keepdims=True)
    weights_ref[...] = weights

    sources = [[jnp.zeros((rx, ry), F32) for _ in range(STEPS)] for _ in range(3)]
    for k in range(nf):
        w = weights[k:k + 1, 0:1]
        for c in range(3):
            re = w * mis[0, k, c]
            im = w * mis[1, k, c]
            for t in range(STEPS):
                sources[c][t] = sources[c][t] + (cos_ref[k, t] * re - sin_ref[k, t] * im)
    for c in range(3):
        for t in range(STEPS):
            near_source[1, 1, t * 3 + c, :, 0:ry] = sources[c][t]
    spread(near_source, 3)
    mixed = jnp.sum(weights * pair_ref[...], axis=0, keepdims=True)

    gathered(near_source, 3)
    shape = (3 * rx, LANES)
    wide_row = lax.broadcasted_iota(jnp.int32, shape, 0)
    wide_lane = lax.broadcasted_iota(jnp.int32, shape, 1)
    on_grid = ((wide_row >= rx) | (gx > 0)) & ((wide_lane < LANES - 4) | (gy > 0))
    nothing = jnp.zeros(shape, F32)
    electric = [[nothing] * (spans + 2) for _ in range(3)]
    magnetic = [[nothing] * (spans + 2) for _ in range(3)]

    def up_x(v):
        return pltpu.roll(v, 3 * rx - 1, 0) - v

    def up_y(v):
        return pltpu.roll(v, LANES - 1, 1) - v

    def down_x(v):
        return v - pltpu.roll(v, 1, 0)

    def down_y(v):
        return v - pltpu.roll(v, 1, 1)

    for t in range(STEPS):
        ex, ey, ez = electric
        for j in range(reach - t + 1, reach + t + 1):
            curls = (
                up_y(ez[j]) - (ey[j + 1] - ey[j]),
                (ex[j + 1] - ex[j]) - up_x(ez[j]),
                up_x(ey[j]) - up_y(ex[j]),
            )
            for c in range(3):
                magnetic[c][j] = jnp.where(on_grid, magnetic[c][j] - courant * curls[c], 0.0)
        mx, my, mz = magnetic
        for j in range(reach - t + 1, reach + t + 2):
            if t > 0:
                s = scales[j - 1]
                curls = (
                    down_y(mz[j]) - (my[j] - my[j - 1]),
                    (mx[j] - mx[j - 1]) - down_x(mz[j]),
                    down_x(my[j]) - down_y(mx[j]),
                )
                for c in range(3):
                    electric[c][j] = electric[c][j] + s * curls[c]
            for c in range(3):
                if j == reach + 1:
                    electric[c][j] = electric[c][j] + widen(lambda a, b: near_source[a, b, t * 3 + c])
                first = (j - 1) * rx
                reply[t * 3 + c, first: first + rx, :] = electric[c][j][rx: 2 * rx, :]

    def turn(n):
        return jnp.concatenate([reply[n, pl.ds(i, 8, stride=rx), :] for i in range(rx)], 0)

    for n in range(0, 3 * STEPS, 2):
        pair = jnp.concatenate([turn(n), turn(n + 1)], 0)
        reply_t[n // 2] = jnp.transpose(pair)[0:ry, :]
    reached = (lane >= z_low) & (lane < z_low + spans)

    def add_reply(t):
        for c in range(3):
            n = t * 3 + c
            for i in range(rx):
                shift = lax.rem(z_low - ((n % 2) * 8 * rx + 8 * i) + 2 * LANES, LANES)
                extra = pltpu.roll(reply_t[n // 2], shift, 1)
                es[1, t + 1, c, i] = es[1, t + 1, c, i] + jnp.where(reached, extra, 0.0)

    for run in range(2):
        for t in range(STEPS):
            for kind in range(2):
                finish(run, t, kind)
    add_reply(STEPS - 1)
    stores[1].start()
    for t in range(STEPS - 1):
        add_reply(t)

    def correlate(s):
        lane_row = lax.broadcasted_iota(jnp.int32, (1, LANES), 1)
        factors = [
            jnp.sum(jnp.where(lane_row == t * STEPS + s, mixed, 0.0), axis=1, keepdims=True)
            for t in range(STEPS)
        ]

        def one(i, carry):
            total = sens[i]
            for c in range(3):
                mix = factors[0] * es[0, 1, c, i]
                for t in range(1, STEPS):
                    mix = mix + factors[t] * es[0, t + 1, c, i]
                total = total + mix * es[1, s + 1, c, i]
            sens[i] = total
            return carry

        lax.fori_loop(0, rx, one, 0, unroll=True)

    for s in range(STEPS):
        correlate(s)

    total = jnp.zeros((ry, nz), F32)
    for i in range(rx):
        value = jnp.sum(jnp.where(in_slab, sens[i], 0.0), axis=1, keepdims=True)
        total = jnp.where(lane == i, value, total)
    gbuf[...] = jnp.zeros_like(gbuf)
    gbuf[:, 0:ry] = jnp.transpose(total)
    density = gbuf[0:rx, :] / float(3 * DZ)
    fx[1, 1, 1] = slope * density
    spread(fx.at[1], 1)
    gathered(fx.at[1], 1)
    grad_ref[...] = smooth(widen(lambda a, b: fx[1, a, b]))[:, 0:ry]

    for store in stores:
        store.wait()


def body(
    nx, ny, e_start, h_start, adj_e_start, adj_h_start, eps_background, design, design_tiles,
    design_floor, freq_index, target,
):
    rx, ry, nz = e_start.shape[1:]
    nf = freq_index.shape[0]
    angular = 0.3 + 0.04 * freq_index.astype(F32)
    times = jnp.arange(1, STEPS + 1, dtype=F32)
    phase = angular[:, None] * times[None, :]
    cosines, sines = jnp.cos(phase), jnp.sin(phase)
    pairs = cosines[:, :, None] * cosines[:, None, :] - sines[:, :, None] * sines[:, None, :]
    pairs = jnp.pad(pairs.reshape(nf, STEPS * STEPS), ((0, 0), (0, LANES - STEPS * STEPS)))
    smem = pl.BlockSpec(memory_space=pltpu.SMEM)
    vmem = pl.BlockSpec(memory_space=pltpu.VMEM)
    hbm = pl.BlockSpec(memory_space=pltpu.HBM)
    field = jax.ShapeDtypeStruct((3, rx, ry, nz), F32)
    slots = 4 * STEPS
    grad, weights, e_final, adj_e_final = pl.pallas_call(
        functools.partial(kernel, nx, ny, nf, rx, ry, nz),
        out_shape=(
            jax.ShapeDtypeStruct((rx, ry), F32),
            jax.ShapeDtypeStruct((nf, LANES), F32),
            field,
            field,
        ),
        in_specs=[smem, smem, smem, smem, vmem, vmem, vmem] + [hbm] * 5,
        out_specs=(vmem, vmem, hbm, hbm),
        scratch_shapes=[
            pltpu.VMEM((2, STEPS + 1, 3, rx, ry, nz), F32),
            pltpu.VMEM((2, STEPS + 1, 3, rx, ry, nz), F32),
            pltpu.VMEM((rx, ry, nz), F32),
            pltpu.VMEM((rx, ry, nz), F32),
            pltpu.VMEM((slots, 2, ry, nz), F32),
            pltpu.VMEM((slots, 2, rx, 8, nz), F32),
            pltpu.VMEM((ry, LANES), F32),
            pltpu.VMEM((LANES, ry), F32),
            pltpu.VMEM((rx, ry, nz), F32),
            pltpu.VMEM((2, nf, 3, rx, ry), F32),
            pltpu.VMEM((2, 3, 3, rx, LANES), F32),
            pltpu.VMEM((3, 3, 2 * STEPS - 1, rx, LANES), F32),
            pltpu.VMEM((3, 3, 3 * STEPS, rx, LANES), F32),
            pltpu.VMEM((3 * STEPS, 8 * rx, LANES), F32),
            pltpu.VMEM((3 * STEPS // 2, ry, LANES), F32),
            pltpu.VMEM((nx, nf, LANES), F32),
            pltpu.VMEM((ny, nf, LANES), F32),
            pltpu.VMEM((LANES, LANES), F32),
            pltpu.SemaphoreType.DMA((5,)),
            pltpu.SemaphoreType.DMA((2,)),
            pltpu.SemaphoreType.DMA((slots, 3)),
            pltpu.SemaphoreType.DMA((slots, 3)),
            pltpu.SemaphoreType.DMA((4, 8)),
            pltpu.SemaphoreType.DMA((4, 8)),
            pltpu.SemaphoreType.DMA((2, max(nx, ny))),
            pltpu.SemaphoreType.DMA((2, max(nx, ny))),
        ],
        compiler_params=pltpu.CompilerParams(
            collective_id=0, has_side_effects=True, vmem_limit_bytes=62 << 20
        ),
    )(
        design_floor, design_tiles, cosines, sines, pairs, design, target,
        e_start, h_start, adj_e_start, adj_h_start, eps_background,
    )
    return grad, weights[:, 0], e_final, adj_e_final


def solution(mesh):
    placed = (
        P(None, "gx", "gy", None),
        P(None, "gx", "gy", None),
        P(None, "gx", "gy", None),
        P(None, "gx", "gy", None),
        P("gx", "gy", None),
        P("gx", "gy"),
        P("gx", "gy"),
        P(),
        P(),
        P(None, None, None, "gx", "gy"),
    )
    return jax.shard_map(
        functools.partial(body, mesh.shape["gx"], mesh.shape["gy"]),
        mesh=mesh,
        in_specs=placed,
        out_specs=(P("gx", "gy"), P(), P(None, "gx", "gy", None), P(None, "gx", "gy", None)),
        check_vma=False,
    )
```

```python
import functools

import jax
import jax.numpy as jnp
from jax import lax
from jax.experimental import pallas as pl
from jax.experimental.pallas import tpu as pltpu
from jax.sharding import PartitionSpec as P

STEPS = 4
DZ = 16
TILE = 8
LANES = 128

courant = 0.5
sharpness = 4.0
contrast = 10.0
threshold = 0.5

MESH = pl.DeviceIdType.MESH
F32 = jnp.float32


def when(cond):
    return pl.when(cond)


def kernel(
    nx, ny, nf, rx, ry, nz,
    floor_ref, tiles_ref, cos_ref, sin_ref, pair_ref, design_ref, target_ref,
    e_in, h_in, ae_in, ah_in, eps_in,
    grad_ref, weights_ref, e_out, ae_out,
    es, hs, eps, scale, hx, hy, plane, planes_t, sens, mis,
    fx, near_scale, near_source, last_source, reply, reply_t, part_x, part_y, gbuf,
    in_sem, out_sem, ssem, rsem, fsend, frecv, psend, precv,
):
    gx = lax.axis_index("gx")
    gy = lax.axis_index("gy")

    loads = [
        pltpu.make_async_copy(e_in, es.at[0, 0], in_sem.at[0]),
        pltpu.make_async_copy(ae_in, es.at[1, 0], in_sem.at[1]),
        pltpu.make_async_copy(h_in, hs.at[0, 0], in_sem.at[2]),
        pltpu.make_async_copy(ah_in, hs.at[1, 0], in_sem.at[3]),
        pltpu.make_async_copy(eps_in, eps, in_sem.at[4]),
    ]
    for load in loads:
        load.start()

    barrier = pltpu.get_barrier_semaphore()
    hx[...] = jnp.zeros_like(hx)
    hy[...] = jnp.zeros_like(hy)
    fx[...] = jnp.zeros_like(fx)
    near_scale[...] = jnp.zeros_like(near_scale)
    near_source[...] = jnp.zeros_like(near_source)
    last_source[...] = jnp.zeros_like(last_source)
    reply[...] = jnp.zeros_like(reply)
    for k in range(1, nx):
        pl.semaphore_signal(barrier, inc=1, device_id=(lax.rem(gx + k, nx), gy), device_id_type=MESH)
    for k in range(1, ny):
        pl.semaphore_signal(barrier, inc=1, device_id=(gx, lax.rem(gy + k, ny)), device_id_type=MESH)

    corners = [(dx, dy) for dx in (-1, 1) for dy in (-1, 1)]
    around = [(-1, 0), (1, 0), (0, -1), (0, 1)] + corners

    def there(dx, dy):
        return (gx + dx >= 0) & (gx + dx < nx) & (gy + dy >= 0) & (gy + dy < ny)

    for dx, dy in corners:
        @when(there(dx, dy))
        def _():
            pl.semaphore_signal(barrier, inc=1, device_id=(gx + dx, gy + dy), device_id_type=MESH)

    row = lax.broadcasted_iota(jnp.int32, (ry, nz), 0)
    lane = lax.broadcasted_iota(jnp.int32, (ry, nz), 1)
    z0 = floor_ref[0]
    at_monitor = lane == z0 + DZ
    in_slab = (lane >= z0) & (lane < z0 + DZ)

    def copies(run, t, kind):
        slot = run * 2 * STEPS + 2 * t + kind
        if kind == 0:
            src, layer, rows, dx, dy = es.at[run, t], 0, pl.ds(0, 8), gx - 1, gy - 1
        else:
            src, layer, rows, dx, dy = hs.at[run, t + 1], rx - 1, pl.ds(ry - 8, 8), gx + 1, gy + 1
        in_x = lambda: pltpu.make_async_remote_copy(
            src.at[pl.ds(1, 2), layer], hx.at[slot], ssem.at[slot, 0], rsem.at[slot, 0],
            device_id=(dx, gy), device_id_type=MESH)
        in_y = lambda: [
            pltpu.make_async_remote_copy(
                src.at[2 * j, :, rows], hy.at[slot, j], ssem.at[slot, 1 + j], rsem.at[slot, 1 + j],
                device_id=(gx, dy), device_id_type=MESH)
            for j in range(2)
        ]
        return in_x, in_y

    low = (gx > 0, gy > 0)
    high = (gx < nx - 1, gy < ny - 1)

    def send_x(run, t, kind):
        @when((low, high)[kind][0])
        def _():
            copies(run, t, kind)[0]().start()

    def send_y(run, t, kind):
        @when((low, high)[kind][1])
        def _():
            for copy in copies(run, t, kind)[1]():
                copy.start()

    def receive(run, t, kind):
        @when((high, low)[kind][0])
        def _():
            copies(run, t, kind)[0]().wait_recv()

        @when((high, low)[kind][1])
        def _():
            for copy in copies(run, t, kind)[1]():
                copy.wait_recv()

    def finish(run, t, kind):
        @when((low, high)[kind][0])
        def _():
            copies(run, t, kind)[0]().wait_send()

        @when((low, high)[kind][1])
        def _():
            for copy in copies(run, t, kind)[1]():
                copy.wait_send()

    def next_y(v, face):
        return jnp.where(row == ry - 1, face, pltpu.roll(v, ry - 1, 0))

    def next_z(v):
        return jnp.where(lane == nz - 1, 0.0, pltpu.roll(v, nz - 1, 1))

    def last_y(v, face):
        return jnp.where(row == 0, face, pltpu.roll(v, 1, 0))

    def last_z(v):
        return jnp.where(lane == 0, 0.0, pltpu.roll(v, 1, 1))

    def h_layer(run, t, i, ey_next, ez_next):
        slot = run * 2 * STEPS + 2 * t
        ex, ey, ez = (es[run, t, c, i] for c in range(3))
        face_x, face_z = hy[slot, 0, i, 0:1, :], hy[slot, 1, i, 0:1, :]
        hs[run, t + 1, 0, i] = hs[run, t, 0, i] - courant * (
            (next_y(ez, face_z) - ez) - (next_z(ey) - ey))
        hs[run, t + 1, 1, i] = hs[run, t, 1, i] - courant * ((next_z(ex) - ex) - (ez_next - ez))
        hs[run, t + 1, 2, i] = hs[run, t, 2, i] - courant * (
            (ey_next - ey) - (next_y(ex, face_x) - ex))

    def h_step(run, t):
        slot = run * 2 * STEPS + 2 * t
        receive(run, t, 0)
        h_layer(run, t, rx - 1, hx[slot, 0], hx[slot, 1])
        send_x(run, t, 1)

        def inner(i, carry):
            h_layer(run, t, i, es[run, t, 1, i + 1], es[run, t, 2, i + 1])
            return carry

        lax.fori_loop(0, rx - 1, inner, 0, unroll=True)
        send_y(run, t, 1)

    def column(t, c, i):
        return lane == (c * STEPS + t) * rx + i

    def e_layer(run, t, i, hy_last, hz_last):
        slot = run * 2 * STEPS + 2 * t + 1
        mx, my, mz = (hs[run, t + 1, c, i] for c in range(3))
        face_x, face_z = hy[slot, 0, i, 7:8, :], hy[slot, 1, i, 7:8, :]
        s = scale[i]
        new = [
            es[run, t, 0, i] + s * ((mz - last_y(mz, face_z)) - (my - last_z(my))),
            es[run, t, 1, i] + s * ((mx - last_z(mx)) - (mz - hz_last)),
            es[run, t, 2, i] + s * ((my - hy_last) - (mx - last_y(mx, face_x))),
        ]
        for c in range(3):
            es[run, t + 1, c, i] = new[c]

    def e_step(run, t, send):
        slot = run * 2 * STEPS + 2 * t + 1
        receive(run, t, 1)
        e_layer(run, t, 0, hx[slot, 0], hx[slot, 1])
        if send:
            send_x(run, t + 1, 0)

        def inner(i, carry):
            e_layer(run, t, i, hs[run, t + 1, 1, i - 1], hs[run, t + 1, 2, i - 1])
            return carry

        lax.fori_loop(1, rx, inner, 0, unroll=True)
        if send:
            send_y(run, t + 1, 0)

    def watch(t):
        def one(i, carry):
            total = plane[...]
            for c in range(3):
                value = jnp.sum(jnp.where(at_monitor, es[0, t + 1, c, i], 0.0), axis=1, keepdims=True)
                total = jnp.where(column(t, c, i), value, total)
            plane[...] = total
            return carry

        lax.fori_loop(0, rx, one, 0, unroll=True)

    def spread_copy(buf, which, n):
        dx, dy = around[n]
        return pltpu.make_async_remote_copy(
            buf.at[1, 1], buf.at[1 - dx, 1 - dy], fsend.at[which, n], frecv.at[which, n],
            device_id=(gx + dx, gy + dy), device_id_type=MESH)

    def spread(buf, which):
        for n, (dx, dy) in enumerate(around):
            @when(there(dx, dy))
            def _():
                spread_copy(buf, which, n).start()

    def gathered(buf, which):
        for n, (dx, dy) in enumerate(around):
            @when(there(-dx, -dy))
            def _():
                spread_copy(buf, which, n).wait_recv()

            @when(there(dx, dy))
            def _():
                spread_copy(buf, which, n).wait_send()

    plane_lane = lax.broadcasted_iota(jnp.int32, (rx, LANES), 1)

    def widen(block, half=0):
        def at(v, moved):
            return pltpu.roll(v, ry, 1) if moved else v

        rows = []
        for a in range(3):
            below = at(block(a, 0), half == 0)
            above = at(block(a, 2), half == 0)
            rows.append(jnp.where(plane_lane < ry, at(block(a, 1), half == 1),
                        jnp.where(plane_lane < ry + 4, above,
                        jnp.where(plane_lane >= LANES - 4, below, 0.0))))
        return jnp.concatenate(rows, 0)

    def pack(buf, planes):
        planes = planes + [jnp.zeros((rx, ry), F32)] * (len(planes) % 2)
        for n in range(0, len(planes), 2):
            buf[1, 1, n // 2] = jnp.concatenate([planes[n], planes[n + 1]], 1)

    def unpack(buf, n):
        return widen(lambda a, b: buf[a, b, n // 2], n % 2)

    def smooth(wide):
        taps = [wide[rx - 2 + d: 2 * rx - 2 + d] for d in range(5)]
        first = (taps[0] + 2.0 * taps[1] + 3.0 * taps[2] + 2.0 * taps[3] + taps[4]) / 9.0
        taps = [first if d == 2 else pltpu.roll(first, (2 - d) % LANES, 1) for d in range(5)]
        return (taps[0] + 2.0 * taps[1] + 3.0 * taps[2] + 2.0 * taps[3] + taps[4]) / 9.0

    beside_x = (gx > 0).astype(jnp.int32) + (gx < nx - 1).astype(jnp.int32)
    beside_y = (gy > 0).astype(jnp.int32) + (gy < ny - 1).astype(jnp.int32)
    pl.semaphore_wait(barrier, nx - 1 + ny - 1 + beside_x * beside_y)
    gbuf[...] = jnp.zeros_like(gbuf)
    gbuf[0:rx, 0:ry] = design_ref[...]
    fx[0, 1, 1] = gbuf[0:rx, :]
    spread(fx.at[0], 0)
    plane[...] = jnp.zeros_like(plane)
    sens[...] = jnp.zeros_like(sens)
    for run in range(2):
        loads[run].wait()
        send_x(run, 0, 0)
        send_y(run, 0, 0)
    loads[2].wait()
    h_step(0, 0)
    loads[3].wait()
    h_step(1, 0)

    gathered(fx.at[0], 0)
    filtered = smooth(widen(lambda a, b: fx[0, a, b]))
    tilted = jnp.tanh(sharpness * (filtered - threshold))
    offset_tanh = jnp.tanh(jnp.full((1, 1), sharpness * threshold, F32))
    projected = (offset_tanh + tilted) / (2.0 * offset_tanh)
    slope = sharpness * (1.0 - tilted * tilted) / (2.0 * offset_tanh)
    cells = jnp.zeros((rx, LANES), F32)
    for a in range(rx // TILE):
        for b in range(ry // TILE):
            x_of = lax.broadcasted_iota(jnp.int32, (rx, LANES), 0)
            here = (x_of // TILE == a) & (plane_lane // TILE == b)
            cells = jnp.where(here, tiles_ref[a, b].astype(F32), cells)
    gbuf[0:rx, :] = jnp.where(cells > 0.5, 1.0 + contrast * projected, -1.0)
    chosen = jnp.transpose(gbuf[...])[0:ry, :]
    slope = slope * cells
    loads[4].wait()
    for i in range(rx):
        value = jnp.sum(jnp.where(lane == i, chosen, 0.0), axis=1, keepdims=True)
        permittivity = jnp.where(in_slab & (value > 0.0), value, eps[i])
        scale[i] = courant / permittivity

    e_step(0, 0, True)
    e_step(1, 0, True)
    watch(0)

    reach = STEPS - 1
    spans = 2 * reach + 1
    z_low = z0 + DZ - reach
    total = jnp.zeros((ry, nz), F32)
    for j in range(spans):
        for i in range(rx):
            value = jnp.sum(jnp.where(lane == z_low + j, scale[i], 0.0), axis=1, keepdims=True)
            total = jnp.where(lane == j * rx + i, value, total)
    planes_t[...] = jnp.transpose(total)
    pack(near_scale, [planes_t[j * rx: (j + 1) * rx, :] for j in range(spans)])
    spread(near_scale, 2)

    def both(t, carry):
        h_step(0, t)
        h_step(1, t)
        e_step(0, t, True)
        e_step(1, t, True)
        watch(t)
        return carry

    lax.fori_loop(1, STEPS - 1, both, 0)
    h_step(0, STEPS - 1)
    h_step(1, STEPS - 1)
    e_step(0, STEPS - 1, False)
    watch(STEPS - 1)
    stores = [pltpu.make_async_copy(es.at[0, STEPS], e_out, out_sem.at[0]),
              pltpu.make_async_copy(es.at[1, STEPS], ae_out, out_sem.at[1])]
    stores[0].start()

    planes_t[...] = jnp.transpose(plane[...])

    def monitor(c, t):
        first = (c * STEPS + t) * rx
        return planes_t[first: first + rx, :]

    shown = [[monitor(c, t) for t in range(STEPS)] for c in range(3)]
    k_row = lax.broadcasted_iota(jnp.int32, (nf, LANES), 0)
    part = jnp.zeros((nf, LANES), F32)
    for k in range(nf):
        square = jnp.zeros((rx, ry), F32)
        for c in range(3):
            re = -target_ref[0, k, c]
            im = -target_ref[1, k, c]
            for t in range(STEPS):
                re = re + cos_ref[k, t] * shown[c][t]
                im = im - sin_ref[k, t] * shown[c][t]
            mis[0, k, c] = re
            mis[1, k, c] = im
            square = square + (re * re + im * im)
        total = jnp.sum(jnp.sum(square, axis=0, keepdims=True), axis=1, keepdims=True)
        part = jnp.where(k_row == k, total, part)

    def gathers(buf, axis):
        me, n = (gx, nx) if axis == 0 else (gy, ny)
        out = []
        for k in range(1, n):
            other = lax.rem(me + k, n)
            out.append(pltpu.make_async_remote_copy(
                buf.at[me], buf.at[me], psend.at[axis, k], precv.at[axis, k],
                device_id=(other, gy) if axis == 0 else (gx, other), device_id_type=MESH))
        return out

    def gather_start(buf, axis, value):
        buf[(gx, gy)[axis]] = value
        for copy in gathers(buf, axis):
            copy.start()

    def gather_sum(buf, axis):
        for copy in gathers(buf, axis):
            copy.wait()
        total = buf[0]
        for k in range(1, (nx, ny)[axis]):
            total = total + buf[k]
        return total

    gather_start(part_x, 0, part)
    e_step(1, STEPS - 1, False)
    gather_start(part_y, 1, gather_sum(part_x, 0))
    gathered(near_scale, 2)
    scales = [unpack(near_scale, j) for j in range(spans)]
    loss_sums = gather_sum(part_y, 1)
    losses = loss_sums / float(3 * rx * nx * ry * ny) + 1e-06
    squared = losses * losses
    weights = squared / jnp.sum(squared, axis=0, keepdims=True)
    weights_ref[...] = weights

    sources = [[jnp.zeros((rx, ry), F32) for _ in range(STEPS)] for _ in range(3)]
    for k in range(nf):
        w = weights[k:k + 1, 0:1]
        for c in range(3):
            re = w * mis[0, k, c]
            im = w * mis[1, k, c]
            for t in range(STEPS):
                sources[c][t] = sources[c][t] + (cos_ref[k, t] * re - sin_ref[k, t] * im)
    pack(near_source, [sources[c][t] for t in range(STEPS - 1) for c in range(3)])
    for c in range(3):
        last_source[c, :, 0:ry] = sources[c][STEPS - 1]
    spread(near_source, 3)
    mixed = jnp.sum(weights * pair_ref[...], axis=0, keepdims=True)

    gathered(near_source, 3)
    shape = (3 * rx, LANES)
    wide_row = lax.broadcasted_iota(jnp.int32, shape, 0)
    wide_lane = lax.broadcasted_iota(jnp.int32, shape, 1)
    on_grid = ((wide_row >= rx) | (gx > 0)) & ((wide_lane < LANES - 4) | (gy > 0))
    nothing = jnp.zeros(shape, F32)
    electric = [[nothing] * (spans + 2) for _ in range(3)]
    magnetic = [[nothing] * (spans + 2) for _ in range(3)]

    def up_x(v):
        return pltpu.roll(v, 3 * rx - 1, 0) - v

    def up_y(v):
        return pltpu.roll(v, LANES - 1, 1) - v

    def down_x(v):
        return v - pltpu.roll(v, 1, 0)

    def down_y(v):
        return v - pltpu.roll(v, 1, 1)

    for t in range(STEPS):
        ex, ey, ez = electric
        for j in range(reach - t + 1, reach + t + 1):
            curls = (
                up_y(ez[j]) - (ey[j + 1] - ey[j]),
                (ex[j + 1] - ex[j]) - up_x(ez[j]),
                up_x(ey[j]) - up_y(ex[j]),
            )
            for c in range(3):
                magnetic[c][j] = jnp.where(on_grid, magnetic[c][j] - courant * curls[c], 0.0)
        mx, my, mz = magnetic
        for j in range(reach - t + 1, reach + t + 2):
            if t > 0:
                s = scales[j - 1]
                curls = (
                    down_y(mz[j]) - (my[j] - my[j - 1]),
                    (mx[j] - mx[j - 1]) - down_x(mz[j]),
                    down_x(my[j]) - down_y(mx[j]),
                )
                for c in range(3):
                    electric[c][j] = electric[c][j] + s * curls[c]
            for c in range(3):
                if j == reach + 1:
                    if t < STEPS - 1:
                        added = unpack(near_source, t * 3 + c)
                    else:
                        added = jnp.concatenate([nothing[0:rx], last_source[c], nothing[0:rx]], 0)
                    electric[c][j] = electric[c][j] + added
                first = (j - 1) * rx
                reply[t * 3 + c, first: first + rx, :] = electric[c][j][rx: 2 * rx, :]

    def turn(n):
        return jnp.concatenate([reply[n, pl.ds(i, 8, stride=rx), :] for i in range(rx)], 0)

    for n in range(0, 3 * STEPS, 2):
        pair = jnp.concatenate([turn(n), turn(n + 1)], 0)
        reply_t[n // 2] = jnp.transpose(pair)[0:ry, :]
    reached = (lane >= z_low) & (lane < z_low + spans)

    def add_reply(t):
        for c in range(3):
            n = t * 3 + c
            for i in range(rx):
                shift = lax.rem(z_low - ((n % 2) * 8 * rx + 8 * i) + 2 * LANES, LANES)
                extra = pltpu.roll(reply_t[n // 2], shift, 1)
                es[1, t + 1, c, i] = es[1, t + 1, c, i] + jnp.where(reached, extra, 0.0)

    for run in range(2):
        for t in range(STEPS):
            for kind in range(2):
                finish(run, t, kind)
    add_reply(STEPS - 1)
    stores[1].start()
    for t in range(STEPS - 1):
        add_reply(t)

    def correlate(s):
        lane_row = lax.broadcasted_iota(jnp.int32, (1, LANES), 1)
        factors = [
            jnp.sum(jnp.where(lane_row == t * STEPS + s, mixed, 0.0), axis=1, keepdims=True)
            for t in range(STEPS)
        ]

        def one(i, carry):
            total = sens[i]
            for c in range(3):
                mix = factors[0] * es[0, 1, c, i]
                for t in range(1, STEPS):
                    mix = mix + factors[t] * es[0, t + 1, c, i]
                total = total + mix * es[1, s + 1, c, i]
            sens[i] = total
            return carry

        lax.fori_loop(0, rx, one, 0, unroll=True)

    for s in range(STEPS):
        correlate(s)

    total = jnp.zeros((ry, nz), F32)
    for i in range(rx):
        value = jnp.sum(jnp.where(in_slab, sens[i], 0.0), axis=1, keepdims=True)
        total = jnp.where(lane == i, value, total)
    gbuf[...] = jnp.zeros_like(gbuf)
    gbuf[:, 0:ry] = jnp.transpose(total)
    density = gbuf[0:rx, :] / float(3 * DZ)
    fx[1, 1, 1] = slope * density
    spread(fx.at[1], 1)
    gathered(fx.at[1], 1)
    grad_ref[...] = smooth(widen(lambda a, b: fx[1, a, b]))[:, 0:ry]

    for store in stores:
        store.wait()


def body(
    nx, ny, e_start, h_start, adj_e_start, adj_h_start, eps_background, design, design_tiles,
    design_floor, freq_index, target,
):
    rx, ry, nz = e_start.shape[1:]
    nf = freq_index.shape[0]
    angular = 0.3 + 0.04 * freq_index.astype(F32)
    times = jnp.arange(1, STEPS + 1, dtype=F32)
    phase = angular[:, None] * times[None, :]
    cosines, sines = jnp.cos(phase), jnp.sin(phase)
    pairs = cosines[:, :, None] * cosines[:, None, :] - sines[:, :, None] * sines[:, None, :]
    pairs = jnp.pad(pairs.reshape(nf, STEPS * STEPS), ((0, 0), (0, LANES - STEPS * STEPS)))
    smem = pl.BlockSpec(memory_space=pltpu.SMEM)
    vmem = pl.BlockSpec(memory_space=pltpu.VMEM)
    kept = pl.BlockSpec(memory_space=pl.ANY)
    hbm = pl.BlockSpec(memory_space=pltpu.HBM)
    field = jax.ShapeDtypeStruct((3, rx, ry, nz), F32)
    slots = 4 * STEPS
    grad, weights, e_final, adj_e_final = pl.pallas_call(
        functools.partial(kernel, nx, ny, nf, rx, ry, nz),
        out_shape=(
            jax.ShapeDtypeStruct((rx, ry), F32),
            jax.ShapeDtypeStruct((nf, LANES), F32),
            field,
            field,
        ),
        in_specs=[smem, smem, smem, smem, vmem, vmem, vmem] + [hbm] * 5,
        out_specs=(vmem, vmem, kept, kept),
        scratch_shapes=[
            pltpu.VMEM((2, STEPS + 1, 3, rx, ry, nz), F32),
            pltpu.VMEM((2, STEPS + 1, 3, rx, ry, nz), F32),
            pltpu.VMEM((rx, ry, nz), F32),
            pltpu.VMEM((rx, ry, nz), F32),
            pltpu.VMEM((slots, 2, ry, nz), F32),
            pltpu.VMEM((slots, 2, rx, 8, nz), F32),
            pltpu.VMEM((ry, LANES), F32),
            pltpu.VMEM((LANES, ry), F32),
            pltpu.VMEM((rx, ry, nz), F32),
            pltpu.VMEM((2, nf, 3, rx, ry), F32),
            pltpu.VMEM((2, 3, 3, rx, LANES), F32),
            pltpu.VMEM((3, 3, STEPS, rx, LANES), F32),
            pltpu.VMEM((3, 3, (3 * STEPS - 2) // 2, rx, LANES), F32),
            pltpu.VMEM((3, rx, LANES), F32),
            pltpu.VMEM((3 * STEPS, 8 * rx, LANES), F32),
            pltpu.VMEM((3 * STEPS // 2, ry, LANES), F32),
            pltpu.VMEM((nx, nf, LANES), F32),
            pltpu.VMEM((ny, nf, LANES), F32),
            pltpu.VMEM((LANES, LANES), F32),
            pltpu.SemaphoreType.DMA((5,)),
            pltpu.SemaphoreType.DMA((2,)),
            pltpu.SemaphoreType.DMA((slots, 3)),
            pltpu.SemaphoreType.DMA((slots, 3)),
            pltpu.SemaphoreType.DMA((4, 8)),
            pltpu.SemaphoreType.DMA((4, 8)),
            pltpu.SemaphoreType.DMA((2, max(nx, ny))),
            pltpu.SemaphoreType.DMA((2, max(nx, ny))),
        ],
        compiler_params=pltpu.CompilerParams(
            collective_id=0, has_side_effects=True, vmem_limit_bytes=62 << 20
        ),
    )(
        design_floor, design_tiles, cosines, sines, pairs, design, target,
        e_start, h_start, adj_e_start, adj_h_start, eps_background,
    )
    return grad, weights[:, 0], e_final, adj_e_final


def solution(mesh):
    placed = (
        P(None, "gx", "gy", None),
        P(None, "gx", "gy", None),
        P(None, "gx", "gy", None),
        P(None, "gx", "gy", None),
        P("gx", "gy", None),
        P("gx", "gy"),
        P("gx", "gy"),
        P(),
        P(),
        P(None, None, None, "gx", "gy"),
    )
    return jax.shard_map(
        functools.partial(body, mesh.shape["gx"], mesh.shape["gy"]),
        mesh=mesh,
        in_specs=placed,
        out_specs=(P("gx", "gy"), P(), P(None, "gx", "gy", None), P(None, "gx", "gy", None)),
        check_vma=False,
    )
```
